32 devices in a mesh: pipe: 4 (over y, x), ctx: 8 (over z, core).
Axes of the slice: x: 2, y: 2, z: 4, core: 2. Of those that a mesh axis runs over, the one named last changes fastest.
Arguments:
- queries: bfloat16 [4, 1, 1024, 3072], P('pipe', None, 'ctx'), may hold values from -24 to 24
- projected_key_value: bfloat16 [4, 1, 1024, 1024], P('pipe', None, 'ctx'), may hold values from -24 to 24
- layout: int32 [1, 1, 16], replicated, may hold values from 0 to 15, each once within a row
Outputs:
- arrived: bfloat16 [4, 1, 1024, 3072], P('pipe', None, 'ctx')
The draws below stay inside these ranges and needn't reach their ends.
Inputs may be any that keep to these rules, and one draw needn't show every extreme that they name: Every row of layout names each of the 16 token blocks once.
All inputs are finite; a program needn't handle non-finite values.
Results may differ from the reference program's by a relative error of at most 0.0055.
Values may be sent and summed in bfloat16 or wider, within the bound.
A program may use at most 64 MiB of HBM per device.

```python
import math
import jax
import jax.numpy as jnp
from jax import lax

HQ = 24
KEY_VALUE_HEADS = 4
HEAD_SIZE = 128
QUERY_PER_KV = 6
TOK_DEV = 128
MICRO_BATCHES = 1
SEQ_DEVS = 8
MICRO_SEQUENCES = 1
BLOCKS = 16
RELAY_SECTIONS = 4
MICRO_TOKENS = 1024


def joint_draw(key):
    query_layout_shape = (RELAY_SECTIONS, MICRO_BATCHES, MICRO_TOKENS, KEY_VALUE_HEADS, QUERY_PER_KV, HEAD_SIZE)
    key_layout_shape = (RELAY_SECTIONS, MICRO_BATCHES, MICRO_TOKENS, KEY_VALUE_HEADS, HEAD_SIZE)
    base_q = jnp.clip(jax.random.normal(jax.random.fold_in(key, 11), query_layout_shape, jnp.float32), -4.0, 4.0)
    base_k = jnp.clip(jax.random.normal(jax.random.fold_in(key, 12), key_layout_shape, jnp.float32), -4.0, 4.0)
    value_portion = jnp.clip(jax.random.normal(jax.random.fold_in(key, 13), key_layout_shape, jnp.float32), -4.0, 4.0)
    query_part = base_q
    key_portion = base_k
    query_flat = query_part.reshape(RELAY_SECTIONS, MICRO_BATCHES, MICRO_TOKENS, HQ * HEAD_SIZE)
    key_value_flat = jnp.concatenate([key_portion.reshape(RELAY_SECTIONS, MICRO_BATCHES, MICRO_TOKENS, KEY_VALUE_HEADS * HEAD_SIZE), value_portion.reshape(RELAY_SECTIONS, MICRO_BATCHES, MICRO_TOKENS, KEY_VALUE_HEADS * HEAD_SIZE)], axis=-1)
    return (query_flat, key_value_flat)


def draw_queries(key, part):
    return joint_draw(key)[0].astype(jnp.bfloat16)


def draw_projected_key_value(key, part):
    return joint_draw(key)[1].astype(jnp.bfloat16)


def setup_inputs(seed: int = 0) -> dict:
    splits = jax.random.split(jax.random.key(seed), 4)
    return {
        "queries": draw_queries(jax.random.fold_in(splits[3], 71), 0),
        "projected_key_value": draw_projected_key_value(jax.random.fold_in(splits[3], 71), 0),
        "layout": jax.vmap(lambda own: jax.random.permutation(own, BLOCKS))(jax.random.split(splits[2], MICRO_BATCHES * MICRO_SEQUENCES)).reshape((MICRO_BATCHES, MICRO_SEQUENCES, BLOCKS)).astype(jnp.int32),
    }


def reference(queries, projected_key_value, layout):
    block_rows = TOK_DEV // 2
    portion_length = SEQ_DEVS * TOK_DEV
    score_scale = 1.0 / math.sqrt(HEAD_SIZE)
    row_iota = jnp.arange(portion_length, dtype=jnp.int32)
    slot_index = row_iota // block_rows
    offsets = row_iota % block_rows
    positions = layout[:, :, slot_index] * block_rows + offsets[None, None, :]
    reshaped_query = queries.reshape(RELAY_SECTIONS, MICRO_BATCHES, MICRO_SEQUENCES, portion_length, KEY_VALUE_HEADS, QUERY_PER_KV, HEAD_SIZE)
    reshaped_key_value = projected_key_value.reshape(RELAY_SECTIONS, MICRO_BATCHES, MICRO_SEQUENCES, portion_length, 2, KEY_VALUE_HEADS, HEAD_SIZE)

    def single(flat_index):
        section = flat_index // (MICRO_BATCHES * MICRO_SEQUENCES)
        micro = flat_index // MICRO_SEQUENCES % MICRO_BATCHES
        sequence = flat_index % MICRO_SEQUENCES
        query_tile_rows = reshaped_query[section, micro, sequence].astype(jnp.float32)
        key_tile_rows = reshaped_key_value[section, micro, sequence, :, 0].astype(jnp.float32)
        value_tile_rows = reshaped_key_value[section, micro, sequence, :, 1].astype(jnp.float32)
        seq_pos = positions[micro, sequence]
        scores = jnp.einsum('ihgd,jhd->hgij', query_tile_rows, key_tile_rows) * score_scale
        allowed = seq_pos[None, :] <= seq_pos[:, None]
        scores = jnp.where(allowed[None, None], scores, -1e+30)
        row_max = lax.optimization_barrier(jnp.max(scores, axis=3))
        expo = jnp.exp(scores - row_max[..., None])
        totals = lax.optimization_barrier(jnp.sum(expo, axis=3))
        weights = expo.astype(jnp.bfloat16).astype(jnp.float32)
        numer = jnp.einsum('hgij,jhd->ihgd', weights, value_tile_rows)
        result = numer / jnp.transpose(totals, (2, 0, 1))[..., None]
        return result.astype(jnp.bfloat16).reshape(portion_length, HQ * HEAD_SIZE)
    outputs = lax.map(single, jnp.arange(RELAY_SECTIONS * MICRO_BATCHES * MICRO_SEQUENCES, dtype=jnp.int32))
    attended = outputs.reshape(RELAY_SECTIONS, MICRO_BATCHES, MICRO_TOKENS, HQ * HEAD_SIZE)
    return jnp.roll(attended, 1, axis=0)
```

```python
import functools
import math

import jax
import jax.numpy as jnp
from jax import lax
from jax.experimental import pallas as pl
from jax.experimental.pallas import tpu as pltpu
from jax.sharding import PartitionSpec as P

HEAD_SIZE = 128
MESH = pl.DeviceIdType.MESH
SHIP = 2
LEAD = 2
CHUNK = 3
OWN_WAVES = (1, 3)
RIGHT, LEFT, SIBLING, FAR_RIGHT, FAR_LEFT = range(5)


def kernel(
    n, sections, key_heads, per_kv,
    layout_hbm, q_hbm, kv_hbm, out_ref,
    q_buf, kv_all, att, bias, eye, layout_ref,
    local_sem, send_sem, recv_sem, out_send, out_recv, ship_send, ship_recv,
):
    rows = q_buf.shape[0]
    block = rows // 2
    chips = n // 2
    section = lax.axis_index("pipe")
    me = lax.axis_index("ctx")
    place = me // 2
    core = me % 2
    width = key_heads * HEAD_SIZE
    stay = key_heads - min(SHIP, key_heads - 1)
    head_width = per_kv * HEAD_SIZE
    after = (section + 1) % sections
    before = (section + sections - 1) % sections
    sibling = 2 * place + 1 - core

    def at_ctx(index):
        return {"pipe": section, "ctx": index}

    def at_pipe(index):
        return {"pipe": index, "ctx": me}

    def sends(way, distance):
        near = jnp.logical_or(distance == 0, distance >= 2)
        if way == RIGHT:
            return jnp.logical_and(
                place + 1 < chips, jnp.logical_or(near, place + 1 == chips - 1)
            )
        if way == LEFT:
            return jnp.logical_and(place >= 1, jnp.logical_or(near, place == 1))
        if way == FAR_RIGHT:
            return jnp.logical_and(distance == 0, place + 2 <= chips - 2)
        return jnp.logical_and(distance == 0, place >= 3)

    barrier = pltpu.get_barrier_semaphore()
    pl.semaphore_signal(barrier, inc=1, device_id=at_pipe(before), device_id_type=MESH)
    senders = (
        (place + 1 < chips, 2),
        (place >= 1, -2),
        (jnp.logical_and(place >= 1, place + 2 < chips), 4),
        (jnp.logical_and(place >= 2, place <= chips - 2), -4),
    )
    for holds, offset in senders:
        @pl.when(holds)
        def _(offset=offset):
            pl.semaphore_signal(
                barrier, inc=1, device_id=at_ctx(me + offset), device_id_type=MESH
            )
    pl.semaphore_signal(barrier, inc=1, device_id=at_ctx(sibling), device_id_type=MESH)

    def own_copy(head, half):
        return pltpu.make_async_copy(
            kv_hbm.at[:, pl.ds(half * width + head * HEAD_SIZE, HEAD_SIZE)],
            kv_all.at[head, me, :, pl.ds(half * HEAD_SIZE, HEAD_SIZE)],
            local_sem.at[2 * head + half],
        )

    q_columns = pl.ds(0, stay * head_width)
    q_copy = pltpu.make_async_copy(
        q_hbm.at[:, q_columns], q_buf.at[:, q_columns], local_sem.at[2 * key_heads]
    )
    layout_copy = pltpu.make_async_copy(layout_hbm, layout_ref, local_sem.at[2 * key_heads + 1])
    for head in range(stay):
        own_copy(head, 0).start()
        own_copy(head, 1).start()
    layout_copy.start()
    q_copy.start()

    def ship_copy(head, what):
        if what == 2:
            columns = pl.ds(head * head_width, head_width)
            source, target = q_hbm.at[:, columns], q_buf.at[:, columns]
        else:
            source = kv_hbm.at[:, pl.ds(what * width + head * HEAD_SIZE, HEAD_SIZE)]
            target = kv_all.at[head, me, :, pl.ds(what * HEAD_SIZE, HEAD_SIZE)]
        return pltpu.make_async_remote_copy(
            src_ref=source,
            dst_ref=target,
            send_sem=ship_send.at[head, what],
            recv_sem=ship_recv.at[head, what],
            device_id=at_pipe(after),
            device_id_type=MESH,
        )

    def piece(head, origin, way):
        target = (me + 2, me - 2, sibling, me + 4, me - 4)[way]
        return pltpu.make_async_remote_copy(
            src_ref=kv_all.at[head, origin],
            dst_ref=kv_all.at[head, origin],
            send_sem=send_sem.at[way, head, origin],
            recv_sem=recv_sem.at[head, origin],
            device_id=at_ctx(target),
            device_id_type=MESH,
        )

    def send_own(head):
        if head >= stay:
            ship_copy(head, 0).wait_recv()
            ship_copy(head, 1).wait_recv()
        for way in (RIGHT, LEFT, FAR_RIGHT, FAR_LEFT):
            @pl.when(sends(way, 0))
            def _(way=way):
                piece(head, me, way).start()
        piece(head, me, SIBLING).start()

    def arrive(head, distance):
        for holds, origin, way in (
            (place >= distance, me - 2 * distance, RIGHT),
            (place + distance < chips, me + 2 * distance, LEFT),
        ):
            @pl.when(holds)
            def _(origin=origin, way=way):
                piece(head, origin, SIBLING).wait_recv()

                @pl.when(sends(way, distance))
                def _():
                    piece(head, origin, way).start()

                piece(head, origin, SIBLING).start()

    pl.semaphore_wait(
        barrier,
        2
        + (place + 1 < chips).astype(jnp.int32)
        + (place >= 1).astype(jnp.int32)
        + (place + 2 <= chips - 2).astype(jnp.int32)
        + (place >= 3).astype(jnp.int32),
    )
    for head in range(stay, key_heads):
        ship_copy(head, 0).start()
        ship_copy(head, 1).start()
    for head in range(stay):
        own_copy(head, 0).wait()
        own_copy(head, 1).wait()
    for head in range(min(LEAD, stay)):
        send_own(head)
    for head in range(stay, key_heads):
        ship_copy(head, 2).start()

    layout_copy.wait()
    row_in = lax.broadcasted_iota(jnp.int32, (rows, rows), 0)
    col_in = lax.broadcasted_iota(jnp.int32, (rows, rows), 1)

    def positions(owner, iota):
        first = layout_ref[0, 0, 2 * owner]
        second = layout_ref[0, 0, 2 * owner + 1]
        return jnp.where(iota < block, first * block + iota, (second - 1) * block + iota)

    query_pos = positions(me, col_in)

    def fill_bias(owner, c):
        key_pos = positions(owner, row_in)
        bias[owner] = jnp.where(key_pos <= query_pos, 0.0, -1e30).astype(jnp.bfloat16)
        return c

    lax.fori_loop(0, n, fill_bias, 0)
    eye[...] = jnp.where(row_in == col_in, 1.0, 0.0).astype(jnp.bfloat16)
    q_copy.wait()

    chunks = per_kv // CHUNK
    factor = math.log2(math.e) / math.sqrt(HEAD_SIZE)

    def chunk_columns(head, chunk):
        return pl.ds((head * per_kv + chunk * CHUNK) * HEAD_SIZE, CHUNK * HEAD_SIZE)

    def out_copy(head, chunk):
        columns = chunk_columns(head, chunk)
        return pltpu.make_async_remote_copy(
            src_ref=att.at[:, columns],
            dst_ref=out_ref.at[:, columns],
            send_sem=out_send.at[head * chunks + chunk],
            recv_sem=out_recv.at[head * chunks + chunk],
            device_id=at_pipe(after),
            device_id_type=MESH,
        )

    def scores_of(head, chunk, first, count):
        keys = kv_all[head, pl.ds(first, count), :, :HEAD_SIZE].reshape(count * rows, HEAD_SIZE)
        masks = bias[pl.ds(first, count)].reshape(count * rows, rows)
        one = eye[...]
        columns = [(head * per_kv + chunk * CHUNK + i) * HEAD_SIZE for i in range(CHUNK)]
        queries = jnp.concatenate(
            [jnp.concatenate([q_buf[:, c:c + HEAD_SIZE], one], axis=1) for c in columns], axis=0
        )
        return lax.dot_general(
            queries, jnp.concatenate([keys, masks], axis=1),
            (((1,), (1,)), ((), ())), preferred_element_type=jnp.float32,
        )

    def weigh(head, scores, row_max, first, count):
        values = kv_all[head, pl.ds(first, count), :, HEAD_SIZE:].reshape(count * rows, HEAD_SIZE)
        weights = jnp.exp2((scores - row_max) * factor).astype(jnp.bfloat16)
        return jnp.dot(
            weights, jnp.concatenate([values, jnp.ones_like(values)], axis=1),
            preferred_element_type=jnp.float32,
        )

    def store(target, head, chunk, product):
        result = (product[:, :HEAD_SIZE] / product[:, HEAD_SIZE:]).astype(jnp.bfloat16)
        for i in range(CHUNK):
            column = (head * per_kv + chunk * CHUNK + i) * HEAD_SIZE
            target[:, column:column + HEAD_SIZE] = result[i * rows:(i + 1) * rows]

    def collect(head, first, count):
        def wait(chip, c):
            piece(head, 2 * chip + 1 - core, SIBLING).wait_recv()
            return c

        lax.fori_loop(first, first + count, wait, 0)

    def attend(head, target):
        scores = scores_of(head, 0, 0, n)
        for chunk in range(chunks):
            later = scores_of(head, chunk + 1, 0, n) if chunk + 1 < chunks else None
            product = weigh(head, scores, jnp.max(scores, axis=1, keepdims=True), 0, n)
            store(target, head, chunk, product)
            if target is att:
                out_copy(head, chunk).start()
            scores = later

    far_chip = jnp.where(2 * place < chips, chips - 1, 0)
    near_chip = jnp.where(2 * place < chips, 0, 1)

    def attend_near(head):
        first, count = 2 * near_chip, 2 * (chips - 1)
        parts = []
        scores = scores_of(head, 0, first, count)
        for chunk in range(chunks):
            later = scores_of(head, chunk + 1, first, count) if chunk + 1 < chunks else None
            row_max = jnp.max(scores, axis=1, keepdims=True)
            parts.append((row_max, weigh(head, scores, row_max, first, count)))
            scores = later
        return parts

    def attend_far(head, parts, target):
        first, count = 2 * far_chip, 2
        scores = [scores_of(head, chunk, first, count) for chunk in range(chunks)]
        for chunk in range(chunks):
            near_max, near_product = parts[chunk]
            row_max = jnp.maximum(near_max, jnp.max(scores[chunk], axis=1, keepdims=True))
            product = near_product * jnp.exp2((near_max - row_max) * factor)
            product = product + weigh(head, scores[chunk], row_max, first, count)
            store(target, head, chunk, product)

    last = key_heads - 1
    parts = None
    for wave in range(1, 2 * last + chips):
        for head in reversed(range(key_heads)):
            distance = wave - 2 * head
            if not 1 <= distance <= chips - 1:
                continue
            if head == last and distance == chips - 1:
                if last >= stay:
                    ship_copy(last, 2).wait_recv()
                collect(last, near_chip, chips - 1)
                parts = attend_near(last)
            arrive(head, distance)
            if distance == chips - 1:
                if head == last:
                    collect(last, far_chip, 1)
                    attend_far(last, parts, out_ref)
                else:
                    if head >= stay:
                        ship_copy(head, 2).wait_recv()
                    collect(head, 0, chips)
                    attend(head, att if head < stay else out_ref)
        for index, head in enumerate(range(min(LEAD, stay), key_heads)):
            if OWN_WAVES[index] == wave:
                send_own(head)

    for head in range(key_heads):
        def finish(chip, c, head=head):
            origin = 2 * chip + core
            gap = place - chip
            for way, holds, distance in (
                (RIGHT, gap >= 0, gap),
                (FAR_RIGHT, gap >= 0, gap),
                (LEFT, gap <= 0, -gap),
                (FAR_LEFT, gap <= 0, -gap),
            ):
                @pl.when(jnp.logical_and(holds, sends(way, distance)))
                def _(way=way):
                    piece(head, origin, way).wait_send()

            piece(head, origin, SIBLING).wait_send()
            return c

        lax.fori_loop(0, chips, finish, 0)

    for head in range(stay, key_heads):
        for what in range(3):
            ship_copy(head, what).wait_send()
    for head in range(stay):
        for chunk in range(chunks):
            out_copy(head, chunk).wait()


def write(parts, source, target, sem):
    share = source.shape[0] // parts
    copies = [
        pltpu.make_async_copy(
            source.at[pl.ds(i * share, share)], target.at[pl.ds(i * share, share)], sem.at[i]
        )
        for i in range(parts)
    ]
    for copy in copies:
        copy.start()
    for copy in copies:
        copy.wait()


def vmem_bytes(n, rows, width, kv_width):
    keys = n * rows
    gathered = 2 * keys * kv_width
    scores = 4 * rows * keys
    return gathered + 3 * 2 * rows * width + (5 * CHUNK + 2) * scores + 4 * 1024 * 1024


def on_device(queries, projected_key_value, layout):
    rows, width = queries.shape[2:]
    kv_width = projected_key_value.shape[3]
    key_heads = kv_width // (2 * HEAD_SIZE)
    per_kv = width // (key_heads * HEAD_SIZE)
    n = lax.axis_size("ctx")
    sections = lax.axis_size("pipe")
    pieces = key_heads * per_kv // CHUNK
    arrived = pl.pallas_call(
        functools.partial(kernel, n, sections, key_heads, per_kv),
        out_shape=jax.ShapeDtypeStruct((rows, width), jnp.bfloat16),
        in_specs=[pl.BlockSpec(memory_space=pltpu.HBM)] * 3,
        out_specs=pl.BlockSpec(memory_space=pltpu.VMEM),
        scratch_shapes=[
            pltpu.VMEM((rows, width), jnp.bfloat16),
            pltpu.VMEM((key_heads, n, rows, 2 * HEAD_SIZE), jnp.bfloat16),
            pltpu.VMEM((rows, width), jnp.bfloat16),
            pltpu.VMEM((n, rows, rows), jnp.bfloat16),
            pltpu.VMEM((rows, rows), jnp.bfloat16),
            pltpu.SMEM(layout.shape, jnp.int32),
            pltpu.SemaphoreType.DMA((2 * key_heads + 2,)),
            pltpu.SemaphoreType.DMA((5, key_heads, n)),
            pltpu.SemaphoreType.DMA((key_heads, n)),
            pltpu.SemaphoreType.DMA((pieces,)),
            pltpu.SemaphoreType.DMA((pieces,)),
            pltpu.SemaphoreType.DMA((key_heads, 3)),
            pltpu.SemaphoreType.DMA((key_heads, 3)),
        ],
        compiler_params=pltpu.CompilerParams(
            collective_id=0, has_side_effects=True, vmem_limit_bytes=vmem_bytes(n, rows, width, kv_width)
        ),
        name="gather_attend_relay",
    )(
        pltpu.with_memory_space_constraint(layout, pltpu.HBM),
        pltpu.with_memory_space_constraint(queries.reshape(rows, width), pltpu.HBM),
        pltpu.with_memory_space_constraint(
            projected_key_value.reshape(rows, kv_width), pltpu.HBM
        ),
    )
    parts = 8
    out = pl.pallas_call(
        functools.partial(write, parts),
        out_shape=jax.ShapeDtypeStruct((rows, width), jnp.bfloat16),
        in_specs=[pl.BlockSpec(memory_space=pltpu.VMEM)],
        out_specs=pl.BlockSpec(memory_space=pltpu.HBM),
        scratch_shapes=[pltpu.SemaphoreType.DMA((parts,))],
        compiler_params=pltpu.CompilerParams(vmem_limit_bytes=8 * 1024 * 1024),
        name="write_back",
    )(arrived)
    return out.reshape(queries.shape)


def solution(mesh):
    placed = (P("pipe", None, "ctx", None), P("pipe", None, "ctx", None), P())
    return jax.shard_map(
        on_device,
        mesh=mesh,
        in_specs=placed,
        out_specs=P("pipe", None, "ctx", None),
        check_vma=False,
    )
```

```python
import functools
import math

import jax
import jax.numpy as jnp
from jax import lax
from jax.experimental import pallas as pl
from jax.experimental.pallas import tpu as pltpu
from jax.sharding import PartitionSpec as P

HEAD_SIZE = 128
MESH = pl.DeviceIdType.MESH
SHIP = 2
LEAD = 2
CHUNK = 3
OWN_WAVES = (1, 3)
RIGHT, LEFT, SIBLING, FAR_RIGHT, FAR_LEFT = range(5)


def kernel(
    n, sections, key_heads, per_kv,
    layout_hbm, q_hbm, kv_hbm, out_ref,
    q_buf, kv_all, att, bias, eye, layout_ref,
    own_sem, local_sem, send_sem, recv_sem, sibling_recv, out_sem, ship_send, ship_recv,
):
    rows = q_buf.shape[0]
    block = rows // 2
    chips = n // 2
    section = lax.axis_index("pipe")
    me = lax.axis_index("ctx")
    place = me // 2
    core = me % 2
    width = key_heads * HEAD_SIZE
    stay = key_heads - min(SHIP, key_heads - 1)
    head_width = per_kv * HEAD_SIZE
    after = (section + 1) % sections
    before = (section + sections - 1) % sections
    sibling = 2 * place + 1 - core

    def at_ctx(index):
        return {"pipe": section, "ctx": index}

    def at_pipe(index):
        return {"pipe": index, "ctx": me}

    def sends(way, distance):
        near = jnp.logical_or(distance == 0, distance >= 2)
        if way == RIGHT:
            return jnp.logical_and(
                place + 1 < chips, jnp.logical_or(near, place + 1 == chips - 1)
            )
        if way == LEFT:
            return jnp.logical_and(place >= 1, jnp.logical_or(near, place == 1))
        if way == FAR_RIGHT:
            return jnp.logical_and(distance == 0, place + 2 <= chips - 2)
        return jnp.logical_and(distance == 0, place >= 3)

    barrier = pltpu.get_barrier_semaphore()
    pl.semaphore_signal(barrier, inc=1, device_id=at_pipe(before), device_id_type=MESH)
    senders = (
        (place + 1 < chips, 2),
        (place >= 1, -2),
        (jnp.logical_and(place >= 1, place + 2 < chips), 4),
        (jnp.logical_and(place >= 2, place <= chips - 2), -4),
    )
    for holds, offset in senders:
        @pl.when(holds)
        def _(offset=offset):
            pl.semaphore_signal(
                barrier, inc=1, device_id=at_ctx(me + offset), device_id_type=MESH
            )
    pl.semaphore_signal(barrier, inc=1, device_id=at_ctx(sibling), device_id_type=MESH)

    def own_copy(head, half):
        return pltpu.make_async_copy(
            kv_hbm.at[:, pl.ds(half * width + head * HEAD_SIZE, HEAD_SIZE)],
            kv_all.at[head, me, :, pl.ds(half * HEAD_SIZE, HEAD_SIZE)],
            own_sem,
        )

    q_columns = pl.ds(0, stay * head_width)
    q_copy = pltpu.make_async_copy(
        q_hbm.at[:, q_columns], q_buf.at[:, q_columns], local_sem.at[0]
    )
    layout_copy = pltpu.make_async_copy(layout_hbm, layout_ref, local_sem.at[1])
    for head in range(stay):
        own_copy(head, 0).start()
        own_copy(head, 1).start()
    layout_copy.start()
    q_copy.start()

    def ship_copy(head, what):
        if what == 2:
            columns = pl.ds(head * head_width, head_width)
            source, target = q_hbm.at[:, columns], q_buf.at[:, columns]
        else:
            source = kv_hbm.at[:, pl.ds(what * width + head * HEAD_SIZE, HEAD_SIZE)]
            target = kv_all.at[head, me, :, pl.ds(what * HEAD_SIZE, HEAD_SIZE)]
        return pltpu.make_async_remote_copy(
            src_ref=source,
            dst_ref=target,
            send_sem=ship_send,
            recv_sem=ship_recv.at[head - stay, what // 2],
            device_id=at_pipe(after),
            device_id_type=MESH,
        )

    last = key_heads - 1
    far_chip = jnp.where(2 * place < chips, chips - 1, 0)
    near_chip = jnp.where(2 * place < chips, 0, 1)

    def piece(head, origin, way):
        target = (me + 2, me - 2, sibling, me + 4, me - 4)[way]
        if way == SIBLING:
            late = jnp.logical_and(head == last, origin // 2 == far_chip)
            arrival = sibling_recv.at[jnp.where(late, key_heads, head)]
        else:
            arrival = recv_sem.at[head, origin // 2]
        return pltpu.make_async_remote_copy(
            src_ref=kv_all.at[head, origin],
            dst_ref=kv_all.at[head, origin],
            send_sem=send_sem.at[1 if way == SIBLING else 0],
            recv_sem=arrival,
            device_id=at_ctx(target),
            device_id_type=MESH,
        )

    def pieces(heads, count, sent, arrival):
        block_of = kv_all.at[pl.ds(0, heads), pl.ds(0, count)]
        return pltpu.make_async_remote_copy(
            src_ref=block_of, dst_ref=block_of, send_sem=send_sem.at[sent], recv_sem=arrival,
            device_id=at_ctx(sibling), device_id_type=MESH,
        )

    def wait_shipped(head):
        if head >= stay:
            pltpu.make_async_remote_copy(
                src_ref=kv_all.at[head, me], dst_ref=kv_all.at[head, me], send_sem=ship_send,
                recv_sem=ship_recv.at[head - stay, 0], device_id=at_pipe(after), device_id_type=MESH,
            ).wait_recv()

    def send_own(head):
        wait_shipped(head)
        for way in (RIGHT, LEFT, FAR_RIGHT, FAR_LEFT):
            @pl.when(sends(way, 0))
            def _(way=way):
                piece(head, me, way).start()
        piece(head, me, SIBLING).start()

    far_side = jnp.where(2 * place < chips, 1, -1)

    def arrive(head, distance, sides=(1, -1)):
        for side in sides:
            chip = place + side * far_side * distance
            rightward = side * far_side < 0

            @pl.when(jnp.logical_and(chip >= 0, chip < chips))
            def _(chip=chip, rightward=rightward):
                origin = 2 * chip + core
                piece(head, origin, RIGHT).wait_recv()
                for way, holds in ((RIGHT, rightward), (LEFT, jnp.logical_not(rightward))):
                    @pl.when(jnp.logical_and(sends(way, distance), holds))
                    def _(way=way):
                        piece(head, origin, way).start()

                piece(head, origin, SIBLING).start()

    pl.semaphore_wait(
        barrier,
        2
        + (place + 1 < chips).astype(jnp.int32)
        + (place >= 1).astype(jnp.int32)
        + (place + 2 <= chips - 2).astype(jnp.int32)
        + (place >= 3).astype(jnp.int32),
    )
    for head in range(stay, key_heads):
        ship_copy(head, 0).start()
        ship_copy(head, 1).start()
    own = kv_all.at[pl.ds(0, stay), me]
    pltpu.make_async_copy(own, own, own_sem).wait()
    for head in range(min(LEAD, stay)):
        send_own(head)
    for head in range(stay, key_heads):
        ship_copy(head, 2).start()

    layout_copy.wait()
    row_in = lax.broadcasted_iota(jnp.int32, (rows, rows), 0)
    col_in = lax.broadcasted_iota(jnp.int32, (rows, rows), 1)

    def positions(owner, iota):
        first = layout_ref[0, 0, 2 * owner]
        second = layout_ref[0, 0, 2 * owner + 1]
        return jnp.where(iota < block, first * block + iota, (second - 1) * block + iota)

    query_pos = positions(me, col_in)

    def fill_bias(owner, c):
        key_pos = positions(owner, row_in)
        bias[owner] = jnp.where(key_pos <= query_pos, 0.0, -1e30).astype(jnp.bfloat16)
        return c

    lax.fori_loop(0, n, fill_bias, 0)
    eye[...] = jnp.where(row_in == col_in, 1.0, 0.0).astype(jnp.bfloat16)
    q_copy.wait()

    chunks = per_kv // CHUNK
    factor = math.log2(math.e) / math.sqrt(HEAD_SIZE)

    def chunk_columns(head, chunk):
        return pl.ds((head * per_kv + chunk * CHUNK) * HEAD_SIZE, CHUNK * HEAD_SIZE)

    def out_copy(head, chunk):
        columns = chunk_columns(head, chunk)
        return pltpu.make_async_remote_copy(
            src_ref=att.at[:, columns],
            dst_ref=out_ref.at[:, columns],
            send_sem=out_sem.at[0],
            recv_sem=out_sem.at[1],
            device_id=at_pipe(after),
            device_id_type=MESH,
        )

    def scores_of(head, chunk, first, count):
        keys = kv_all[head, pl.ds(first, count), :, :HEAD_SIZE].reshape(count * rows, HEAD_SIZE)
        masks = bias[pl.ds(first, count)].reshape(count * rows, rows)
        one = eye[...]
        columns = [(head * per_kv + chunk * CHUNK + i) * HEAD_SIZE for i in range(CHUNK)]
        queries = jnp.concatenate(
            [jnp.concatenate([q_buf[:, c:c + HEAD_SIZE], one], axis=1) for c in columns], axis=0
        )
        return lax.dot_general(
            queries, jnp.concatenate([keys, masks], axis=1),
            (((1,), (1,)), ((), ())), preferred_element_type=jnp.float32,
        )

    def weigh(head, scores, row_max, first, count):
        values = kv_all[head, pl.ds(first, count), :, HEAD_SIZE:].reshape(count * rows, HEAD_SIZE)
        weights = jnp.exp2((scores - row_max) * factor).astype(jnp.bfloat16)
        return jnp.dot(
            weights, jnp.concatenate([values, jnp.ones_like(values)], axis=1),
            preferred_element_type=jnp.float32,
        )

    def store(target, head, chunk, product):
        result = (product[:, :HEAD_SIZE] / product[:, HEAD_SIZE:]).astype(jnp.bfloat16)
        for i in range(CHUNK):
            column = (head * per_kv + chunk * CHUNK + i) * HEAD_SIZE
            target[:, column:column + HEAD_SIZE] = result[i * rows:(i + 1) * rows]

    def collect(head, count):
        pieces(1, count, 1, sibling_recv.at[head]).wait_recv()

    def attend(head, target):
        scores = scores_of(head, 0, 0, n)
        for chunk in range(chunks):
            later = scores_of(head, chunk + 1, 0, n) if chunk + 1 < chunks else None
            product = weigh(head, scores, jnp.max(scores, axis=1, keepdims=True), 0, n)
            store(target, head, chunk, product)
            if target is att:
                out_copy(head, chunk).start()
            scores = later

    def attend_near(head):
        first, count = 2 * near_chip, 2 * (chips - 1)
        parts = []
        scores = scores_of(head, 0, first, count)
        for chunk in range(chunks):
            later = scores_of(head, chunk + 1, first, count) if chunk + 1 < chunks else None
            row_max = jnp.max(scores, axis=1, keepdims=True)
            parts.append((row_max, weigh(head, scores, row_max, first, count)))
            scores = later
        return parts

    def attend_far(head, parts, target):
        first, count = 2 * far_chip, 2
        scores = [scores_of(head, chunk, first, count) for chunk in range(chunks)]
        for chunk in range(chunks):
            near_max, near_product = parts[chunk]
            row_max = jnp.maximum(near_max, jnp.max(scores[chunk], axis=1, keepdims=True))
            product = near_product * jnp.exp2((near_max - row_max) * factor)
            product = product + weigh(head, scores[chunk], row_max, first, count)
            store(target, head, chunk, product)

    parts = None
    for wave in range(1, 2 * last + chips):
        for head in reversed(range(key_heads)):
            distance = wave - 2 * head
            if not 1 <= distance <= chips - 1:
                continue
            if head == last and distance == chips - 1:
                if last >= stay:
                    ship_copy(last, 2).wait_recv()
                collect(last, chips - 1)
                parts = attend_near(last)
            arrive(head, distance)
            if distance == chips - 1:
                if head == last:
                    collect(key_heads, 1)
                    attend_far(last, parts, out_ref)
                else:
                    if head >= stay:
                        ship_copy(head, 2).wait_recv()
                    collect(head, chips)
                    attend(head, att if head < stay else out_ref)
        for index, head in enumerate(range(min(LEAD, stay), key_heads)):
            if OWN_WAVES[index] == wave:
                send_own(head)

    total = jnp.int32(0)
    for distance in range(chips):
        for way in (RIGHT, LEFT, FAR_RIGHT, FAR_LEFT):
            chip = place - distance if way in (RIGHT, FAR_RIGHT) else place + distance
            held = jnp.logical_and(chip >= 0, chip < chips)
            total = total + jnp.logical_and(held, sends(way, distance)).astype(jnp.int32)
    for count in range(1, n + 1):
        @pl.when(total == count)
        def _(count=count):
            pieces(key_heads, count, 0, recv_sem.at[0, 0]).wait_send()

    pieces(key_heads, chips, 1, sibling_recv.at[0]).wait_send()
    shipped = q_hbm.at[:, pl.ds(0, (key_heads - stay) * (head_width + 2 * HEAD_SIZE))]
    pltpu.make_async_remote_copy(
        src_ref=shipped, dst_ref=shipped, send_sem=ship_send, recv_sem=ship_recv.at[0, 0],
        device_id=at_pipe(after), device_id_type=MESH,
    ).wait_send()
    done = pl.ds(0, stay * head_width)
    pltpu.make_async_remote_copy(
        src_ref=att.at[:, done], dst_ref=out_ref.at[:, done], send_sem=out_sem.at[0],
        recv_sem=out_sem.at[1], device_id=at_pipe(after), device_id_type=MESH,
    ).wait()


def write(parts, source, target, sem):
    share = source.shape[0] // parts
    copies = [
        pltpu.make_async_copy(
            source.at[pl.ds(i * share, share)], target.at[pl.ds(i * share, share)], sem.at[i]
        )
        for i in range(parts)
    ]
    for copy in copies:
        copy.start()
    for copy in copies:
        copy.wait()


def vmem_bytes(n, rows, width, kv_width):
    keys = n * rows
    gathered = 2 * keys * kv_width
    scores = 4 * rows * keys
    return gathered + 3 * 2 * rows * width + (5 * CHUNK + 2) * scores + 4 * 1024 * 1024


def on_device(queries, projected_key_value, layout):
    rows, width = queries.shape[2:]
    kv_width = projected_key_value.shape[3]
    key_heads = kv_width // (2 * HEAD_SIZE)
    per_kv = width // (key_heads * HEAD_SIZE)
    n = lax.axis_size("ctx")
    sections = lax.axis_size("pipe")
    arrived = pl.pallas_call(
        functools.partial(kernel, n, sections, key_heads, per_kv),
        out_shape=jax.ShapeDtypeStruct((rows, width), jnp.bfloat16),
        in_specs=[pl.BlockSpec(memory_space=pltpu.HBM)] * 3,
        out_specs=pl.BlockSpec(memory_space=pltpu.VMEM),
        scratch_shapes=[
            pltpu.VMEM((rows, width), jnp.bfloat16),
            pltpu.VMEM((key_heads, n, rows, 2 * HEAD_SIZE), jnp.bfloat16),
            pltpu.VMEM((rows, width), jnp.bfloat16),
            pltpu.VMEM((n, rows, rows), jnp.bfloat16),
            pltpu.VMEM((rows, rows), jnp.bfloat16),
            pltpu.SMEM(layout.shape, jnp.int32),
            pltpu.SemaphoreType.DMA,
            pltpu.SemaphoreType.DMA((2,)),
            pltpu.SemaphoreType.DMA((2,)),
            pltpu.SemaphoreType.DMA((key_heads, n // 2)),
            pltpu.SemaphoreType.DMA((key_heads + 1,)),
            pltpu.SemaphoreType.DMA((2,)),
            pltpu.SemaphoreType.DMA,
            pltpu.SemaphoreType.DMA((min(SHIP, key_heads - 1), 2)),
        ],
        compiler_params=pltpu.CompilerParams(
            collective_id=0, has_side_effects=True, vmem_limit_bytes=vmem_bytes(n, rows, width, kv_width)
        ),
        name="gather_attend_relay",
    )(
        pltpu.with_memory_space_constraint(layout, pltpu.HBM),
        pltpu.with_memory_space_constraint(queries.reshape(rows, width), pltpu.HBM),
        pltpu.with_memory_space_constraint(
            projected_key_value.reshape(rows, kv_width), pltpu.HBM
        ),
    )
    parts = 1
    out = pl.pallas_call(
        functools.partial(write, parts),
        out_shape=jax.ShapeDtypeStruct((rows, width), jnp.bfloat16),
        in_specs=[pl.BlockSpec(memory_space=pltpu.VMEM)],
        out_specs=pl.BlockSpec(memory_space=pltpu.HBM),
        scratch_shapes=[pltpu.SemaphoreType.DMA((parts,))],
        compiler_params=pltpu.CompilerParams(vmem_limit_bytes=8 * 1024 * 1024),
        name="write_back",
    )(arrived)
    return out.reshape(queries.shape)


def solution(mesh):
    placed = (P("pipe", None, "ctx", None), P("pipe", None, "ctx", None), P())
    return jax.shard_map(
        on_device,
        mesh=mesh,
        in_specs=placed,
        out_specs=P("pipe", None, "ctx", None),
        check_vma=False,
    )
```

```python
import functools
import math

import jax
import jax.numpy as jnp
from jax import lax
from jax.experimental import pallas as pl
from jax.experimental.pallas import tpu as pltpu
from jax.sharding import PartitionSpec as P

HEAD_SIZE = 128
MESH = pl.DeviceIdType.MESH
SHIP = 2
LEAD = 2
CHUNK = 2
OWN_WAVES = (1, 3)
RIGHT, LEFT, SIBLING, FAR_RIGHT, FAR_LEFT = range(5)


def kernel(
    n, sections, key_heads, per_kv,
    layout_hbm, q_hbm, kv_hbm, out_ref,
    q_buf, kv_all, att, bias, eye, layout_ref,
    own_sem, local_sem, send_sem, recv_sem, sibling_recv, out_sem, ship_send, ship_recv, ready,
):
    rows = q_buf.shape[0]
    block = rows // 2
    chips = n // 2
    section = lax.axis_index("pipe")
    me = lax.axis_index("ctx")
    place = me // 2
    core = me % 2
    width = key_heads * HEAD_SIZE
    stay = key_heads - min(SHIP, key_heads - 1)
    head_width = per_kv * HEAD_SIZE
    after = (section + 1) % sections
    before = (section + sections - 1) % sections
    sibling = 2 * place + 1 - core

    def at_ctx(index):
        return {"pipe": section, "ctx": index}

    def at_pipe(index):
        return {"pipe": index, "ctx": me}

    def sends(way, distance):
        near = jnp.logical_or(distance == 0, distance >= 2)
        if way == RIGHT:
            return jnp.logical_and(
                place + 1 < chips, jnp.logical_or(near, place + 1 == chips - 1)
            )
        if way == LEFT:
            return jnp.logical_and(place >= 1, jnp.logical_or(near, place == 1))
        if way == FAR_RIGHT:
            return jnp.logical_and(distance == 0, place + 2 <= chips - 2)
        return jnp.logical_and(distance == 0, place >= 3)

    barrier = pltpu.get_barrier_semaphore()
    pl.semaphore_signal(barrier, inc=1, device_id=at_pipe(before), device_id_type=MESH)
    senders = (
        (place + 1 < chips, 2),
        (place >= 1, -2),
    )
    for holds, offset in senders:
        @pl.when(holds)
        def _(offset=offset):
            pl.semaphore_signal(
                barrier, inc=1, device_id=at_ctx(me + offset), device_id_type=MESH
            )
    pl.semaphore_signal(barrier, inc=1, device_id=at_ctx(sibling), device_id_type=MESH)

    def own_copy(head, half):
        return pltpu.make_async_copy(
            kv_hbm.at[:, pl.ds(half * width + head * HEAD_SIZE, HEAD_SIZE)],
            kv_all.at[head, me, :, pl.ds(half * HEAD_SIZE, HEAD_SIZE)],
            own_sem,
        )

    q_columns = pl.ds(0, stay * head_width)
    q_copy = pltpu.make_async_copy(
        q_hbm.at[:, q_columns], q_buf.at[:, q_columns], local_sem.at[0]
    )
    layout_copy = pltpu.make_async_copy(layout_hbm, layout_ref, local_sem.at[1])
    for head in range(stay):
        own_copy(head, 0).start()
        own_copy(head, 1).start()
    layout_copy.start()
    q_copy.start()

    def ship_copy(head, what):
        if what == 2:
            columns = pl.ds(head * head_width, head_width)
            source, target = q_hbm.at[:, columns], q_buf.at[:, columns]
        else:
            source = kv_hbm.at[:, pl.ds(what * width + head * HEAD_SIZE, HEAD_SIZE)]
            target = kv_all.at[head, me, :, pl.ds(what * HEAD_SIZE, HEAD_SIZE)]
        return pltpu.make_async_remote_copy(
            src_ref=source,
            dst_ref=target,
            send_sem=ship_send,
            recv_sem=ship_recv.at[head - stay, what // 2],
            device_id=at_pipe(after),
            device_id_type=MESH,
        )

    last = key_heads - 1
    far_chip = jnp.where(2 * place < chips, chips - 1, 0)
    near_chip = jnp.where(2 * place < chips, 0, 1)

    def piece(head, origin, way):
        target = (me + 2, me - 2, sibling, me + 4, me - 4)[way]
        if way == SIBLING:
            late = jnp.logical_and(head == last, origin // 2 == far_chip)
            arrival = sibling_recv.at[jnp.where(late, key_heads, head)]
        else:
            arrival = recv_sem.at[head, origin // 2]
        return pltpu.make_async_remote_copy(
            src_ref=kv_all.at[head, origin],
            dst_ref=kv_all.at[head, origin],
            send_sem=send_sem.at[1 if way == SIBLING else 0],
            recv_sem=arrival,
            device_id=at_ctx(target),
            device_id_type=MESH,
        )

    def pieces(heads, count, sent, arrival):
        block_of = kv_all.at[pl.ds(0, heads), pl.ds(0, count)]
        return pltpu.make_async_remote_copy(
            src_ref=block_of, dst_ref=block_of, send_sem=send_sem.at[sent], recv_sem=arrival,
            device_id=at_ctx(sibling), device_id_type=MESH,
        )

    def wait_shipped(head):
        if head >= stay:
            pltpu.make_async_remote_copy(
                src_ref=kv_all.at[head, me], dst_ref=kv_all.at[head, me], send_sem=ship_send,
                recv_sem=ship_recv.at[head - stay, 0], device_id=at_pipe(after), device_id_type=MESH,
            ).wait_recv()

    def send_own(head):
        wait_shipped(head)
        for ways in ((RIGHT, LEFT), (FAR_RIGHT, FAR_LEFT)):
            if head == 0 and FAR_LEFT in ways:
                wait_far()
            for way in ways:
                @pl.when(sends(way, 0))
                def _(way=way):
                    piece(head, me, way).start()

        piece(head, me, SIBLING).start()

    far_side = jnp.where(2 * place < chips, 1, -1)

    def arrive(head, distance, sides=(1, -1)):
        for side in sides:
            chip = place + side * far_side * distance
            rightward = side * far_side < 0

            @pl.when(jnp.logical_and(chip >= 0, chip < chips))
            def _(chip=chip, rightward=rightward):
                origin = 2 * chip + core
                piece(head, origin, RIGHT).wait_recv()
                for way, holds in ((RIGHT, rightward), (LEFT, jnp.logical_not(rightward))):
                    @pl.when(jnp.logical_and(sends(way, distance), holds))
                    def _(way=way):
                        piece(head, origin, way).start()

                piece(head, origin, SIBLING).start()

    pl.semaphore_wait(
        barrier,
        2
        + (place + 1 < chips).astype(jnp.int32)
        + (place >= 1).astype(jnp.int32),
    )
    for holds, offset in (
        (jnp.logical_and(place >= 1, place + 1 <= chips - 2), -2),
        (jnp.logical_and(place >= 2, place + 1 < chips), 2),
    ):
        @pl.when(holds)
        def _(offset=offset):
            pl.semaphore_signal(
                ready, inc=1, device_id=at_ctx(me + offset), device_id_type=MESH
            )

    def wait_far():
        for way in (FAR_RIGHT, FAR_LEFT):
            @pl.when(sends(way, 0))
            def _():
                pl.semaphore_wait(ready, 1)

    for head in range(stay, key_heads):
        ship_copy(head, 0).start()
        ship_copy(head, 1).start()
    own = kv_all.at[pl.ds(0, stay), me]
    pltpu.make_async_copy(own, own, own_sem).wait()
    for head in range(min(LEAD, stay)):
        send_own(head)
    for head in range(stay, key_heads):
        ship_copy(head, 2).start()

    layout_copy.wait()
    row_in = lax.broadcasted_iota(jnp.int32, (rows, rows), 0)
    col_in = lax.broadcasted_iota(jnp.int32, (rows, rows), 1)

    def positions(owner, iota):
        first = layout_ref[0, 0, 2 * owner]
        second = layout_ref[0, 0, 2 * owner + 1]
        return jnp.where(iota < block, first * block + iota, (second - 1) * block + iota)

    query_pos = positions(me, col_in)

    def fill_bias(owner, c):
        key_pos = positions(owner, row_in)
        bias[owner] = jnp.where(key_pos <= query_pos, 0.0, -1e30).astype(jnp.bfloat16)
        return c

    lax.fori_loop(0, n, fill_bias, 0)
    eye[...] = jnp.where(row_in == col_in, 1.0, 0.0).astype(jnp.bfloat16)
    q_copy.wait()

    chunks = per_kv // CHUNK
    factor = math.log2(math.e) / math.sqrt(HEAD_SIZE)

    def chunk_columns(head, chunk):
        return pl.ds((head * per_kv + chunk * CHUNK) * HEAD_SIZE, CHUNK * HEAD_SIZE)

    def out_copy(head, chunk):
        columns = chunk_columns(head, chunk)
        return pltpu.make_async_remote_copy(
            src_ref=att.at[:, columns],
            dst_ref=out_ref.at[:, columns],
            send_sem=out_sem.at[0],
            recv_sem=out_sem.at[1],
            device_id=at_pipe(after),
            device_id_type=MESH,
        )

    def scores_of(head, chunk, first, count):
        keys = kv_all[head, pl.ds(first, count), :, :HEAD_SIZE].reshape(count * rows, HEAD_SIZE)
        masks = bias[pl.ds(first, count)].reshape(count * rows, rows)
        one = eye[...]
        columns = [(head * per_kv + chunk * CHUNK + i) * HEAD_SIZE for i in range(CHUNK)]
        queries = jnp.concatenate(
            [jnp.concatenate([q_buf[:, c:c + HEAD_SIZE], one], axis=1) for c in columns], axis=0
        )
        return lax.dot_general(
            queries, jnp.concatenate([keys, masks], axis=1),
            (((1,), (1,)), ((), ())), preferred_element_type=jnp.float32,
        )

    def weigh(head, scores, row_max, first, count):
        values = kv_all[head, pl.ds(first, count), :, HEAD_SIZE:].reshape(count * rows, HEAD_SIZE)
        weights = jnp.exp2((scores - row_max) * factor).astype(jnp.bfloat16)
        return jnp.dot(
            weights, jnp.concatenate([values, jnp.ones_like(values)], axis=1),
            preferred_element_type=jnp.float32,
        )

    def store(target, head, chunk, product):
        result = (product[:, :HEAD_SIZE] / product[:, HEAD_SIZE:]).astype(jnp.bfloat16)
        for i in range(CHUNK):
            column = (head * per_kv + chunk * CHUNK + i) * HEAD_SIZE
            target[:, column:column + HEAD_SIZE] = result[i * rows:(i + 1) * rows]

    def collect(head, count):
        pieces(1, count, 1, sibling_recv.at[head]).wait_recv()

    def attend(head, target):
        scores = scores_of(head, 0, 0, n)
        for chunk in range(chunks):
            later = scores_of(head, chunk + 1, 0, n) if chunk + 1 < chunks else None
            product = weigh(head, scores, jnp.max(scores, axis=1, keepdims=True), 0, n)
            store(target, head, chunk, product)
            if target is att:
                out_copy(head, chunk).start()
            scores = later

    def attend_near(head):
        first, count = 2 * near_chip, 2 * (chips - 1)
        parts = []
        scores = scores_of(head, 0, first, count)
        for chunk in range(chunks):
            later = scores_of(head, chunk + 1, first, count) if chunk + 1 < chunks else None
            row_max = jnp.max(scores, axis=1, keepdims=True)
            parts.append((row_max, weigh(head, scores, row_max, first, count)))
            scores = later
        return parts

    def attend_far(head, parts, target):
        first, count = 2 * far_chip, 2
        scores = [scores_of(head, chunk, first, count) for chunk in range(chunks)]
        for chunk in range(chunks):
            near_max, near_product = parts[chunk]
            row_max = jnp.maximum(near_max, jnp.max(scores[chunk], axis=1, keepdims=True))
            product = near_product * jnp.exp2((near_max - row_max) * factor)
            product = product + weigh(head, scores[chunk], row_max, first, count)
            store(target, head, chunk, product)

    parts = None
    for wave in range(1, 2 * last + chips):
        for head in reversed(range(key_heads)):
            distance = wave - 2 * head
            if not 1 <= distance <= chips - 1:
                continue
            if head == last and distance == chips - 1:
                if last >= stay:
                    ship_copy(last, 2).wait_recv()
                collect(last, chips - 1)
                parts = attend_near(last)
            arrive(head, distance)
            if distance == chips - 1:
                if head == last:
                    collect(key_heads, 1)
                    attend_far(last, parts, out_ref)
                else:
                    if head >= stay:
                        ship_copy(head, 2).wait_recv()
                    collect(head, chips)
                    attend(head, att if head < stay else out_ref)
        for index, head in enumerate(range(min(LEAD, stay), key_heads)):
            if OWN_WAVES[index] == wave:
                send_own(head)

    total = jnp.int32(0)
    for distance in range(chips):
        for way in (RIGHT, LEFT, FAR_RIGHT, FAR_LEFT):
            chip = place - distance if way in (RIGHT, FAR_RIGHT) else place + distance
            held = jnp.logical_and(chip >= 0, chip < chips)
            total = total + jnp.logical_and(held, sends(way, distance)).astype(jnp.int32)
    for count in range(1, n + 1):
        @pl.when(total == count)
        def _(count=count):
            pieces(key_heads, count, 0, recv_sem.at[0, 0]).wait_send()

    pieces(key_heads, chips, 1, sibling_recv.at[0]).wait_send()
    shipped = q_hbm.at[:, pl.ds(0, (key_heads - stay) * (head_width + 2 * HEAD_SIZE))]
    pltpu.make_async_remote_copy(
        src_ref=shipped, dst_ref=shipped, send_sem=ship_send, recv_sem=ship_recv.at[0, 0],
        device_id=at_pipe(after), device_id_type=MESH,
    ).wait_send()
    done = pl.ds(0, stay * head_width)
    pltpu.make_async_remote_copy(
        src_ref=att.at[:, done], dst_ref=out_ref.at[:, done], send_sem=out_sem.at[0],
        recv_sem=out_sem.at[1], device_id=at_pipe(after), device_id_type=MESH,
    ).wait()


def write(parts, source, target, sem):
    share = source.shape[0] // parts
    copies = [
        pltpu.make_async_copy(
            source.at[pl.ds(i * share, share)], target.at[pl.ds(i * share, share)], sem.at[i]
        )
        for i in range(parts)
    ]
    for copy in copies:
        copy.start()
    for copy in copies:
        copy.wait()


def vmem_bytes(n, rows, width, kv_width):
    keys = n * rows
    gathered = 2 * keys * kv_width
    scores = 4 * rows * keys
    return gathered + 3 * 2 * rows * width + (5 * CHUNK + 2) * scores + 4 * 1024 * 1024


def on_device(queries, projected_key_value, layout):
    rows, width = queries.shape[2:]
    kv_width = projected_key_value.shape[3]
    key_heads = kv_width // (2 * HEAD_SIZE)
    per_kv = width // (key_heads * HEAD_SIZE)
    n = lax.axis_size("ctx")
    sections = lax.axis_size("pipe")
    arrived = pl.pallas_call(
        functools.partial(kernel, n, sections, key_heads, per_kv),
        out_shape=jax.ShapeDtypeStruct((rows, width), jnp.bfloat16),
        in_specs=[pl.BlockSpec(memory_space=pltpu.HBM)] * 3,
        out_specs=pl.BlockSpec(memory_space=pltpu.VMEM),
        scratch_shapes=[
            pltpu.VMEM((rows, width), jnp.bfloat16),
            pltpu.VMEM((key_heads, n, rows, 2 * HEAD_SIZE), jnp.bfloat16),
            pltpu.VMEM((rows, width), jnp.bfloat16),
            pltpu.VMEM((n, rows, rows), jnp.bfloat16),
            pltpu.VMEM((rows, rows), jnp.bfloat16),
            pltpu.SMEM(layout.shape, jnp.int32),
            pltpu.SemaphoreType.DMA,
            pltpu.SemaphoreType.DMA((2,)),
            pltpu.SemaphoreType.DMA((2,)),
            pltpu.SemaphoreType.DMA((key_heads, n // 2)),
            pltpu.SemaphoreType.DMA((key_heads + 1,)),
            pltpu.SemaphoreType.DMA((2,)),
            pltpu.SemaphoreType.DMA,
            pltpu.SemaphoreType.DMA((min(SHIP, key_heads - 1), 2)),
            pltpu.SemaphoreType.REGULAR,
        ],
        compiler_params=pltpu.CompilerParams(
            collective_id=0, has_side_effects=True, vmem_limit_bytes=vmem_bytes(n, rows, width, kv_width)
        ),
        name="gather_attend_relay",
    )(
        pltpu.with_memory_space_constraint(layout, pltpu.HBM),
        pltpu.with_memory_space_constraint(queries.reshape(rows, width), pltpu.HBM),
        pltpu.with_memory_space_constraint(
            projected_key_value.reshape(rows, kv_width), pltpu.HBM
        ),
    )
    parts = 1
    out = pl.pallas_call(
        functools.partial(write, parts),
        out_shape=jax.ShapeDtypeStruct((rows, width), jnp.bfloat16),
        in_specs=[pl.BlockSpec(memory_space=pltpu.VMEM)],
        out_specs=pl.BlockSpec(memory_space=pltpu.HBM),
        scratch_shapes=[pltpu.SemaphoreType.DMA((parts,))],
        compiler_params=pltpu.CompilerParams(vmem_limit_bytes=8 * 1024 * 1024),
        name="write_back",
    )(arrived)
    return out.reshape(queries.shape)


def solution(mesh):
    placed = (P("pipe", None, "ctx", None), P("pipe", None, "ctx", None), P())
    return jax.shard_map(
        on_device,
        mesh=mesh,
        in_specs=placed,
        out_specs=P("pipe", None, "ctx", None),
        check_vma=False,
    )
```

```python
import functools
import math

import jax
import jax.numpy as jnp
from jax import lax
from jax.experimental import pallas as pl
from jax.experimental.pallas import tpu as pltpu
from jax.sharding import PartitionSpec as P

HEAD_SIZE = 128
MESH = pl.DeviceIdType.MESH
SHIP = 2
LEAD = 2
CHUNK = 3
SPLIT = (1, 3)
OWN_WAVES = (1, 3)
RIGHT, LEFT, SIBLING, FAR_RIGHT, FAR_LEFT = range(5)


def kernel(
    n, sections, key_heads, per_kv,
    layout_hbm, q_hbm, kv_hbm, out_ref,
    q_buf, kv_all, att, bias, eye, layout_ref,
    own_sem, local_sem, send_sem, recv_sem, sibling_recv, out_sem, ship_send, ship_recv, ready,
):
    rows = q_buf.shape[0]
    block = rows // 2
    chips = n // 2
    section = lax.axis_index("pipe")
    me = lax.axis_index("ctx")
    place = me // 2
    core = me % 2
    width = key_heads * HEAD_SIZE
    stay = key_heads - min(SHIP, key_heads - 1)
    head_width = per_kv * HEAD_SIZE
    after = (section + 1) % sections
    before = (section + sections - 1) % sections
    sibling = 2 * place + 1 - core

    def at_ctx(index):
        return {"pipe": section, "ctx": index}

    def at_pipe(index):
        return {"pipe": index, "ctx": me}

    def sends(way, distance):
        near = jnp.logical_or(distance == 0, distance >= 2)
        if way == RIGHT:
            return jnp.logical_and(
                place + 1 < chips, jnp.logical_or(near, place + 1 == chips - 1)
            )
        if way == LEFT:
            return jnp.logical_and(place >= 1, jnp.logical_or(near, place == 1))
        if way == FAR_RIGHT:
            return jnp.logical_and(distance == 0, place + 2 <= chips - 2)
        return jnp.logical_and(distance == 0, place >= 3)

    barrier = pltpu.get_barrier_semaphore()
    pl.semaphore_signal(barrier, inc=1, device_id=at_pipe(before), device_id_type=MESH)
    senders = (
        (place + 1 < chips, 2),
        (place >= 1, -2),
    )
    for holds, offset in senders:
        @pl.when(holds)
        def _(offset=offset):
            pl.semaphore_signal(
                barrier, inc=1, device_id=at_ctx(me + offset), device_id_type=MESH
            )
    pl.semaphore_signal(barrier, inc=1, device_id=at_ctx(sibling), device_id_type=MESH)

    def own_copy(head, half):
        return pltpu.make_async_copy(
            kv_hbm.at[:, pl.ds(half * width + head * HEAD_SIZE, HEAD_SIZE)],
            kv_all.at[head, me, :, pl.ds(half * HEAD_SIZE, HEAD_SIZE)],
            own_sem,
        )

    q_columns = pl.ds(0, stay * head_width)
    q_copy = pltpu.make_async_copy(
        q_hbm.at[:, q_columns], q_buf.at[:, q_columns], local_sem.at[0]
    )
    layout_copy = pltpu.make_async_copy(layout_hbm, layout_ref, local_sem.at[1])
    for head in range(stay):
        own_copy(head, 0).start()
        own_copy(head, 1).start()
    layout_copy.start()
    q_copy.start()

    def ship_copy(head, what):
        if what == 2:
            columns = pl.ds(head * head_width, head_width)
            source, target = q_hbm.at[:, columns], q_buf.at[:, columns]
        else:
            source = kv_hbm.at[:, pl.ds(what * width + head * HEAD_SIZE, HEAD_SIZE)]
            target = kv_all.at[head, me, :, pl.ds(what * HEAD_SIZE, HEAD_SIZE)]
        return pltpu.make_async_remote_copy(
            src_ref=source,
            dst_ref=target,
            send_sem=ship_send,
            recv_sem=ship_recv.at[head - stay, what // 2],
            device_id=at_pipe(after),
            device_id_type=MESH,
        )

    last = key_heads - 1
    far_chip = jnp.where(2 * place < chips, chips - 1, 0)
    near_chip = jnp.where(2 * place < chips, 0, 1)

    def piece(head, origin, way):
        target = (me + 2, me - 2, sibling, me + 4, me - 4)[way]
        if way == SIBLING:
            arrival = sibling_recv.at[head, (origin // 2 == far_chip).astype(jnp.int32)]
        else:
            arrival = recv_sem.at[head, origin // 2]
        return pltpu.make_async_remote_copy(
            src_ref=kv_all.at[head, origin],
            dst_ref=kv_all.at[head, origin],
            send_sem=send_sem.at[1 if way == SIBLING else 0],
            recv_sem=arrival,
            device_id=at_ctx(target),
            device_id_type=MESH,
        )

    def pieces(heads, count, sent, arrival):
        block_of = kv_all.at[pl.ds(0, heads), pl.ds(0, count)]
        return pltpu.make_async_remote_copy(
            src_ref=block_of, dst_ref=block_of, send_sem=send_sem.at[sent], recv_sem=arrival,
            device_id=at_ctx(sibling), device_id_type=MESH,
        )

    def wait_shipped(head):
        if head >= stay:
            pltpu.make_async_remote_copy(
                src_ref=kv_all.at[head, me], dst_ref=kv_all.at[head, me], send_sem=ship_send,
                recv_sem=ship_recv.at[head - stay, 0], device_id=at_pipe(after), device_id_type=MESH,
            ).wait_recv()

    def send_own(head):
        wait_shipped(head)
        for ways in ((RIGHT, LEFT), (FAR_RIGHT, FAR_LEFT)):
            if head == 0 and FAR_LEFT in ways:
                wait_far()
            for way in ways:
                @pl.when(sends(way, 0))
                def _(way=way):
                    piece(head, me, way).start()

        piece(head, me, SIBLING).start()

    far_side = jnp.where(2 * place < chips, 1, -1)

    def arrive(head, distance, sides=(1, -1)):
        for side in sides:
            chip = place + side * far_side * distance
            rightward = side * far_side < 0

            @pl.when(jnp.logical_and(chip >= 0, chip < chips))
            def _(chip=chip, rightward=rightward):
                origin = 2 * chip + core
                piece(head, origin, RIGHT).wait_recv()
                for way, holds in ((RIGHT, rightward), (LEFT, jnp.logical_not(rightward))):
                    @pl.when(jnp.logical_and(sends(way, distance), holds))
                    def _(way=way):
                        piece(head, origin, way).start()

                piece(head, origin, SIBLING).start()

    pl.semaphore_wait(
        barrier,
        2
        + (place + 1 < chips).astype(jnp.int32)
        + (place >= 1).astype(jnp.int32),
    )
    for holds, offset in (
        (jnp.logical_and(place >= 1, place + 1 <= chips - 2), -2),
        (jnp.logical_and(place >= 2, place + 1 < chips), 2),
    ):
        @pl.when(holds)
        def _(offset=offset):
            pl.semaphore_signal(
                ready, inc=1, device_id=at_ctx(me + offset), device_id_type=MESH
            )

    def wait_far():
        for way in (FAR_RIGHT, FAR_LEFT):
            @pl.when(sends(way, 0))
            def _():
                pl.semaphore_wait(ready, 1)

    for head in range(stay, key_heads):
        ship_copy(head, 0).start()
        ship_copy(head, 1).start()
    own = kv_all.at[pl.ds(0, stay), me]
    pltpu.make_async_copy(own, own, own_sem).wait()
    for head in range(min(LEAD, stay)):
        send_own(head)
    for head in range(stay, key_heads):
        ship_copy(head, 2).start()

    layout_copy.wait()
    row_in = lax.broadcasted_iota(jnp.int32, (rows, rows), 0)
    col_in = lax.broadcasted_iota(jnp.int32, (rows, rows), 1)

    def positions(owner, iota):
        first = layout_ref[0, 0, 2 * owner]
        second = layout_ref[0, 0, 2 * owner + 1]
        return jnp.where(iota < block, first * block + iota, (second - 1) * block + iota)

    query_pos = positions(me, col_in)

    def fill_bias(owner, c):
        key_pos = positions(owner, row_in)
        bias[owner] = jnp.where(key_pos <= query_pos, 0.0, -1e30).astype(jnp.bfloat16)
        return c

    lax.fori_loop(0, n, fill_bias, 0)
    eye[...] = jnp.where(row_in == col_in, 1.0, 0.0).astype(jnp.bfloat16)
    q_copy.wait()

    chunks = per_kv // CHUNK
    factor = math.log2(math.e) / math.sqrt(HEAD_SIZE)

    def chunk_columns(head, chunk):
        return pl.ds((head * per_kv + chunk * CHUNK) * HEAD_SIZE, CHUNK * HEAD_SIZE)

    def out_copy(head, chunk):
        columns = chunk_columns(head, chunk)
        return pltpu.make_async_remote_copy(
            src_ref=att.at[:, columns],
            dst_ref=out_ref.at[:, columns],
            send_sem=out_sem.at[0],
            recv_sem=out_sem.at[1],
            device_id=at_pipe(after),
            device_id_type=MESH,
        )

    def scores_of(head, chunk, first, count):
        keys = kv_all[head, pl.ds(first, count), :, :HEAD_SIZE].reshape(count * rows, HEAD_SIZE)
        masks = bias[pl.ds(first, count)].reshape(count * rows, rows)
        one = eye[...]
        columns = [(head * per_kv + chunk * CHUNK + i) * HEAD_SIZE for i in range(CHUNK)]
        queries = jnp.concatenate(
            [jnp.concatenate([q_buf[:, c:c + HEAD_SIZE], one], axis=1) for c in columns], axis=0
        )
        return lax.dot_general(
            queries, jnp.concatenate([keys, masks], axis=1),
            (((1,), (1,)), ((), ())), preferred_element_type=jnp.float32,
        )

    def weigh(head, scores, row_max, first, count):
        values = kv_all[head, pl.ds(first, count), :, HEAD_SIZE:].reshape(count * rows, HEAD_SIZE)
        weights = jnp.exp2((scores - row_max) * factor).astype(jnp.bfloat16)
        return jnp.dot(
            weights, jnp.concatenate([values, jnp.ones_like(values)], axis=1),
            preferred_element_type=jnp.float32,
        )

    def store(target, head, chunk, product):
        result = (product[:, :HEAD_SIZE] / product[:, HEAD_SIZE:]).astype(jnp.bfloat16)
        for i in range(CHUNK):
            column = (head * per_kv + chunk * CHUNK + i) * HEAD_SIZE
            target[:, column:column + HEAD_SIZE] = result[i * rows:(i + 1) * rows]

    def collect(head, count, late):
        pieces(1, count, 1, sibling_recv.at[head, late]).wait_recv()

    def attend(head, target):
        scores = scores_of(head, 0, 0, n)
        for chunk in range(chunks):
            later = scores_of(head, chunk + 1, 0, n) if chunk + 1 < chunks else None
            product = weigh(head, scores, jnp.max(scores, axis=1, keepdims=True), 0, n)
            store(target, head, chunk, product)
            if target is att:
                out_copy(head, chunk).start()
            scores = later

    def attend_near(head):
        first, count = 2 * near_chip, 2 * (chips - 1)
        parts = []
        scores = scores_of(head, 0, first, count)
        for chunk in range(chunks):
            later = scores_of(head, chunk + 1, first, count) if chunk + 1 < chunks else None
            row_max = jnp.max(scores, axis=1, keepdims=True)
            parts.append((row_max, weigh(head, scores, row_max, first, count)))
            scores = later
        return parts

    def attend_far(head, parts, target):
        first, count = 2 * far_chip, 2
        scores = [scores_of(head, chunk, first, count) for chunk in range(chunks)]
        for chunk in range(chunks):
            near_max, near_product = parts[chunk]
            row_max = jnp.maximum(near_max, jnp.max(scores[chunk], axis=1, keepdims=True))
            product = near_product * jnp.exp2((near_max - row_max) * factor)
            product = product + weigh(head, scores[chunk], row_max, first, count)
            store(target, head, chunk, product)
            if target is att:
                out_copy(head, chunk).start()

    for wave in range(1, 2 * last + chips):
        for head in reversed(range(key_heads)):
            distance = wave - 2 * head
            if not 1 <= distance <= chips - 1:
                continue
            if distance == chips - 1:
                if head >= stay:
                    ship_copy(head, 2).wait_recv()
                if head in SPLIT:
                    collect(head, chips - 1, 0)
                    parts = attend_near(head)
            arrive(head, distance)
            if distance == chips - 1:
                target = att if head < stay else out_ref
                if head not in SPLIT:
                    collect(head, chips - 1, 0)
                collect(head, 1, 1)
                if head in SPLIT:
                    attend_far(head, parts, target)
                else:
                    attend(head, target)
        for index, head in enumerate(range(min(LEAD, stay), key_heads)):
            if OWN_WAVES[index] == wave:
                send_own(head)

    total = jnp.int32(0)
    for distance in range(chips):
        for way in (RIGHT, LEFT, FAR_RIGHT, FAR_LEFT):
            chip = place - distance if way in (RIGHT, FAR_RIGHT) else place + distance
            held = jnp.logical_and(chip >= 0, chip < chips)
            total = total + jnp.logical_and(held, sends(way, distance)).astype(jnp.int32)
    for count in range(1, n + 1):
        @pl.when(total == count)
        def _(count=count):
            pieces(key_heads, count, 0, recv_sem.at[0, 0]).wait_send()

    pieces(key_heads, chips, 1, sibling_recv.at[0, 0]).wait_send()
    shipped = q_hbm.at[:, pl.ds(0, (key_heads - stay) * (head_width + 2 * HEAD_SIZE))]
    pltpu.make_async_remote_copy(
        src_ref=shipped, dst_ref=shipped, send_sem=ship_send, recv_sem=ship_recv.at[0, 0],
        device_id=at_pipe(after), device_id_type=MESH,
    ).wait_send()
    done = pl.ds(0, stay * head_width)
    pltpu.make_async_remote_copy(
        src_ref=att.at[:, done], dst_ref=out_ref.at[:, done], send_sem=out_sem.at[0],
        recv_sem=out_sem.at[1], device_id=at_pipe(after), device_id_type=MESH,
    ).wait()


def write(parts, source, target, sem):
    share = source.shape[0] // parts
    copies = [
        pltpu.make_async_copy(
            source.at[pl.ds(i * share, share)], target.at[pl.ds(i * share, share)], sem.at[i]
        )
        for i in range(parts)
    ]
    for copy in copies:
        copy.start()
    for copy in copies:
        copy.wait()


def vmem_bytes(n, rows, width, kv_width):
    keys = n * rows
    gathered = 2 * keys * kv_width
    scores = 4 * rows * keys
    return gathered + 3 * 2 * rows * width + (5 * CHUNK + 2) * scores + 4 * 1024 * 1024


def on_device(queries, projected_key_value, layout):
    rows, width = queries.shape[2:]
    kv_width = projected_key_value.shape[3]
    key_heads = kv_width // (2 * HEAD_SIZE)
    per_kv = width // (key_heads * HEAD_SIZE)
    n = lax.axis_size("ctx")
    sections = lax.axis_size("pipe")
    arrived = pl.pallas_call(
        functools.partial(kernel, n, sections, key_heads, per_kv),
        out_shape=jax.ShapeDtypeStruct((rows, width), jnp.bfloat16),
        in_specs=[pl.BlockSpec(memory_space=pltpu.HBM)] * 3,
        out_specs=pl.BlockSpec(memory_space=pltpu.VMEM),
        scratch_shapes=[
            pltpu.VMEM((rows, width), jnp.bfloat16),
            pltpu.VMEM((key_heads, n, rows, 2 * HEAD_SIZE), jnp.bfloat16),
            pltpu.VMEM((rows, width), jnp.bfloat16),
            pltpu.VMEM((n, rows, rows), jnp.bfloat16),
            pltpu.VMEM((rows, rows), jnp.bfloat16),
            pltpu.SMEM(layout.shape, jnp.int32),
            pltpu.SemaphoreType.DMA,
            pltpu.SemaphoreType.DMA((2,)),
            pltpu.SemaphoreType.DMA((2,)),
            pltpu.SemaphoreType.DMA((key_heads, n // 2)),
            pltpu.SemaphoreType.DMA((key_heads, 2)),
            pltpu.SemaphoreType.DMA((2,)),
            pltpu.SemaphoreType.DMA,
            pltpu.SemaphoreType.DMA((min(SHIP, key_heads - 1), 2)),
            pltpu.SemaphoreType.REGULAR,
        ],
        compiler_params=pltpu.CompilerParams(
            collective_id=0, has_side_effects=True, vmem_limit_bytes=vmem_bytes(n, rows, width, kv_width)
        ),
        name="gather_attend_relay",
    )(
        pltpu.with_memory_space_constraint(layout, pltpu.HBM),
        pltpu.with_memory_space_constraint(queries.reshape(rows, width), pltpu.HBM),
        pltpu.with_memory_space_constraint(
            projected_key_value.reshape(rows, kv_width), pltpu.HBM
        ),
    )
    parts = 1
    out = pl.pallas_call(
        functools.partial(write, parts),
        out_shape=jax.ShapeDtypeStruct((rows, width), jnp.bfloat16),
        in_specs=[pl.BlockSpec(memory_space=pltpu.VMEM)],
        out_specs=pl.BlockSpec(memory_space=pltpu.HBM),
        scratch_shapes=[pltpu.SemaphoreType.DMA((parts,))],
        compiler_params=pltpu.CompilerParams(vmem_limit_bytes=8 * 1024 * 1024),
        name="write_back",
    )(arrived)
    return out.reshape(queries.shape)


def solution(mesh):
    placed = (P("pipe", None, "ctx", None), P("pipe", None, "ctx", None), P())
    return jax.shard_map(
        on_device,
        mesh=mesh,
        in_specs=placed,
        out_specs=P("pipe", None, "ctx", None),
        check_vma=False,
    )
```

```python
import functools
import math

import jax
import jax.numpy as jnp
from jax import lax
from jax.experimental import pallas as pl
from jax.experimental.pallas import tpu as pltpu
from jax.sharding import PartitionSpec as P

HEAD_SIZE = 128
MESH = pl.DeviceIdType.MESH
SHIP = 2
LEAD = 2
CHUNK = 3
SPLIT = (1, 3)
OWN_WAVES = (1, 3)
RIGHT, LEFT, SIBLING, FAR_RIGHT, FAR_LEFT = range(5)


def kernel(
    n, sections, key_heads, per_kv,
    layout_hbm, q_hbm, kv_hbm, out_ref,
    q_buf, kv_all, att, bias, eye, layout_ref,
    own_sem, local_sem, send_sem, recv_sem, sibling_recv, out_sem, ship_send, ship_recv, ready,
):
    rows = q_buf.shape[0]
    block = rows // 2
    chips = n // 2
    section = lax.axis_index("pipe")
    me = lax.axis_index("ctx")
    place = me // 2
    core = me % 2
    width = key_heads * HEAD_SIZE
    stay = key_heads - min(SHIP, key_heads - 1)
    head_width = per_kv * HEAD_SIZE
    after = (section + 1) % sections
    before = (section + sections - 1) % sections
    sibling = 2 * place + 1 - core

    def at_ctx(index):
        return {"pipe": section, "ctx": index}

    def at_pipe(index):
        return {"pipe": index, "ctx": me}

    def sends(way, distance):
        near = jnp.logical_or(distance == 0, distance >= 2)
        if way == RIGHT:
            return jnp.logical_and(
                place + 1 < chips, jnp.logical_or(near, place + 1 == chips - 1)
            )
        if way == LEFT:
            return jnp.logical_and(place >= 1, jnp.logical_or(near, place == 1))
        if way == FAR_RIGHT:
            return jnp.logical_and(distance == 0, place + 2 <= chips - 2)
        return jnp.logical_and(distance == 0, place >= 3)

    barrier = pltpu.get_barrier_semaphore()
    pl.semaphore_signal(barrier, inc=1, device_id=at_pipe(before), device_id_type=MESH)
    senders = (
        (place + 1 < chips, 2),
        (place >= 1, -2),
    )
    for holds, offset in senders:
        @pl.when(holds)
        def _(offset=offset):
            pl.semaphore_signal(
                barrier, inc=1, device_id=at_ctx(me + offset), device_id_type=MESH
            )
    pl.semaphore_signal(barrier, inc=1, device_id=at_ctx(sibling), device_id_type=MESH)

    def own_copy(head, half):
        return pltpu.make_async_copy(
            kv_hbm.at[:, pl.ds(half * width + head * HEAD_SIZE, HEAD_SIZE)],
            kv_all.at[head, me, :, pl.ds(half * HEAD_SIZE, HEAD_SIZE)],
            own_sem,
        )

    q_columns = pl.ds(0, stay * head_width)
    q_copy = pltpu.make_async_copy(
        q_hbm.at[:, q_columns], q_buf.at[:, q_columns], local_sem.at[0]
    )
    layout_copy = pltpu.make_async_copy(layout_hbm, layout_ref, local_sem.at[1])
    for head in range(stay):
        own_copy(head, 0).start()
        own_copy(head, 1).start()
    layout_copy.start()
    q_copy.start()

    def ship_copy(head, what):
        if what == 2:
            columns = pl.ds(stay * head_width, (key_heads - stay) * head_width)
            source, target = q_hbm.at[:, columns], q_buf.at[:, columns]
        else:
            source = kv_hbm.at[:, pl.ds(what * width + head * HEAD_SIZE, HEAD_SIZE)]
            target = kv_all.at[head, me, :, pl.ds(what * HEAD_SIZE, HEAD_SIZE)]
        return pltpu.make_async_remote_copy(
            src_ref=source,
            dst_ref=target,
            send_sem=ship_send,
            recv_sem=ship_recv.at[key_heads - stay if what == 2 else head - stay],
            device_id=at_pipe(after),
            device_id_type=MESH,
        )

    last = key_heads - 1
    far_chip = jnp.where(2 * place < chips, chips - 1, 0)
    near_chip = jnp.where(2 * place < chips, 0, 1)

    def sibling_slot(head):
        return head + sum(other < head for other in SPLIT)

    def piece(head, origin, way):
        target = (me + 2, me - 2, sibling, me + 4, me - 4)[way]
        if way == SIBLING:
            late = (origin // 2 == far_chip).astype(jnp.int32) if head in SPLIT else 0
            arrival = sibling_recv.at[sibling_slot(head) + late]
        else:
            arrival = recv_sem.at[head, origin // 2 - (1 if way in (LEFT, FAR_LEFT) else 0)]
        return pltpu.make_async_remote_copy(
            src_ref=kv_all.at[head, origin],
            dst_ref=kv_all.at[head, origin],
            send_sem=send_sem.at[1 if way == SIBLING else 0],
            recv_sem=arrival,
            device_id=at_ctx(target),
            device_id_type=MESH,
        )

    def pieces(heads, count, sent, arrival):
        block_of = kv_all.at[pl.ds(0, heads), pl.ds(0, count)]
        return pltpu.make_async_remote_copy(
            src_ref=block_of, dst_ref=block_of, send_sem=send_sem.at[sent], recv_sem=arrival,
            device_id=at_ctx(sibling), device_id_type=MESH,
        )

    def wait_shipped(head):
        if head >= stay:
            pltpu.make_async_remote_copy(
                src_ref=kv_all.at[head, me], dst_ref=kv_all.at[head, me], send_sem=ship_send,
                recv_sem=ship_recv.at[head - stay], device_id=at_pipe(after), device_id_type=MESH,
            ).wait_recv()

    def send_own(head):
        wait_shipped(head)
        for ways in ((RIGHT, LEFT), (FAR_RIGHT, FAR_LEFT)):
            if head == 0 and FAR_LEFT in ways:
                wait_far()
            for way in ways:
                @pl.when(sends(way, 0))
                def _(way=way):
                    piece(head, me, way).start()

        piece(head, me, SIBLING).start()

    far_side = jnp.where(2 * place < chips, 1, -1)

    def arrive(head, distance, sides=(1, -1)):
        for side in sides:
            chip = place + side * far_side * distance
            rightward = side * far_side < 0

            @pl.when(jnp.logical_and(chip >= 0, chip < chips))
            def _(chip=chip, rightward=rightward):
                origin = 2 * chip + core
                for way, holds in ((RIGHT, chip < place), (LEFT, chip > place)):
                    @pl.when(holds)
                    def _(way=way):
                        piece(head, origin, way).wait_recv()

                for way, holds in ((RIGHT, rightward), (LEFT, jnp.logical_not(rightward))):
                    @pl.when(jnp.logical_and(sends(way, distance), holds))
                    def _(way=way):
                        piece(head, origin, way).start()

                piece(head, origin, SIBLING).start()

    pl.semaphore_wait(
        barrier,
        2
        + (place + 1 < chips).astype(jnp.int32)
        + (place >= 1).astype(jnp.int32),
    )
    for holds, offset in (
        (jnp.logical_and(place >= 1, place + 1 <= chips - 2), -2),
        (jnp.logical_and(place >= 2, place + 1 < chips), 2),
    ):
        @pl.when(holds)
        def _(offset=offset):
            pl.semaphore_signal(
                ready, inc=1, device_id=at_ctx(me + offset), device_id_type=MESH
            )

    def wait_far():
        for way in (FAR_RIGHT, FAR_LEFT):
            @pl.when(sends(way, 0))
            def _():
                pl.semaphore_wait(ready, 1)

    for head in range(stay, key_heads):
        ship_copy(head, 0).start()
        ship_copy(head, 1).start()
    own = kv_all.at[pl.ds(0, stay), me]
    pltpu.make_async_copy(own, own, own_sem).wait()
    for head in range(min(LEAD, stay)):
        send_own(head)
    ship_copy(stay, 2).start()

    layout_copy.wait()
    row_in = lax.broadcasted_iota(jnp.int32, (rows, rows), 0)
    col_in = lax.broadcasted_iota(jnp.int32, (rows, rows), 1)

    def positions(owner, iota):
        first = layout_ref[0, 0, 2 * owner]
        second = layout_ref[0, 0, 2 * owner + 1]
        return jnp.where(iota < block, first * block + iota, (second - 1) * block + iota)

    query_pos = positions(me, col_in)

    def fill_bias(owner, c):
        key_pos = positions(owner, row_in)
        bias[owner] = jnp.where(key_pos <= query_pos, 0.0, -1e30).astype(jnp.bfloat16)
        return c

    lax.fori_loop(0, n, fill_bias, 0)
    eye[...] = jnp.where(row_in == col_in, 1.0, 0.0).astype(jnp.bfloat16)
    q_copy.wait()

    chunks = per_kv // CHUNK
    factor = math.log2(math.e) / math.sqrt(HEAD_SIZE)

    def chunk_columns(head, chunk):
        return pl.ds((head * per_kv + chunk * CHUNK) * HEAD_SIZE, CHUNK * HEAD_SIZE)

    def out_copy(head, chunk):
        columns = chunk_columns(head, chunk)
        return pltpu.make_async_remote_copy(
            src_ref=att.at[:, columns],
            dst_ref=out_ref.at[:, columns],
            send_sem=out_sem.at[0],
            recv_sem=out_sem.at[1],
            device_id=at_pipe(after),
            device_id_type=MESH,
        )

    def scores_of(head, chunk, first, count):
        keys = kv_all[head, pl.ds(first, count), :, :HEAD_SIZE].reshape(count * rows, HEAD_SIZE)
        masks = bias[pl.ds(first, count)].reshape(count * rows, rows)
        one = eye[...]
        columns = [(head * per_kv + chunk * CHUNK + i) * HEAD_SIZE for i in range(CHUNK)]
        queries = jnp.concatenate(
            [jnp.concatenate([q_buf[:, c:c + HEAD_SIZE], one], axis=1) for c in columns], axis=0
        )
        return lax.dot_general(
            queries, jnp.concatenate([keys, masks], axis=1),
            (((1,), (1,)), ((), ())), preferred_element_type=jnp.float32,
        )

    def weigh(head, scores, row_max, first, count):
        values = kv_all[head, pl.ds(first, count), :, HEAD_SIZE:].reshape(count * rows, HEAD_SIZE)
        weights = jnp.exp2((scores - row_max) * factor).astype(jnp.bfloat16)
        return jnp.dot(
            weights, jnp.concatenate([values, jnp.ones_like(values)], axis=1),
            preferred_element_type=jnp.float32,
        )

    def store(target, head, chunk, product):
        result = (product[:, :HEAD_SIZE] / product[:, HEAD_SIZE:]).astype(jnp.bfloat16)
        for i in range(CHUNK):
            column = (head * per_kv + chunk * CHUNK + i) * HEAD_SIZE
            target[:, column:column + HEAD_SIZE] = result[i * rows:(i + 1) * rows]

    def collect(head, count, late):
        pieces(1, count, 1, sibling_recv.at[sibling_slot(head) + late]).wait_recv()

    def attend(head, target):
        scores = scores_of(head, 0, 0, n)
        for chunk in range(chunks):
            later = scores_of(head, chunk + 1, 0, n) if chunk + 1 < chunks else None
            product = weigh(head, scores, jnp.max(scores, axis=1, keepdims=True), 0, n)
            store(target, head, chunk, product)
            if target is att:
                out_copy(head, chunk).start()
            scores = later

    def attend_near(head):
        first, count = 2 * near_chip, 2 * (chips - 1)
        parts = []
        scores = scores_of(head, 0, first, count)
        for chunk in range(chunks):
            later = scores_of(head, chunk + 1, first, count) if chunk + 1 < chunks else None
            row_max = jnp.max(scores, axis=1, keepdims=True)
            parts.append((row_max, weigh(head, scores, row_max, first, count)))
            scores = later
        return parts

    def attend_far(head, parts, target):
        first, count = 2 * far_chip, 2
        scores = [scores_of(head, chunk, first, count) for chunk in range(chunks)]
        for chunk in range(chunks):
            near_max, near_product = parts[chunk]
            row_max = jnp.maximum(near_max, jnp.max(scores[chunk], axis=1, keepdims=True))
            product = near_product * jnp.exp2((near_max - row_max) * factor)
            product = product + weigh(head, scores[chunk], row_max, first, count)
            store(target, head, chunk, product)
            if target is att:
                out_copy(head, chunk).start()

    for wave in range(1, 2 * last + chips):
        for head in reversed(range(key_heads)):
            distance = wave - 2 * head
            if not 1 <= distance <= chips - 1:
                continue
            if distance == chips - 1:
                if head == stay:
                    ship_copy(head, 2).wait_recv()
                if head in SPLIT:
                    collect(head, chips - 1, 0)
                    parts = attend_near(head)
            arrive(head, distance)
            if distance == chips - 1:
                target = att if head < stay else out_ref
                if head not in SPLIT:
                    collect(head, chips, 0)
                else:
                    collect(head, 1, 1)
                if head in SPLIT:
                    attend_far(head, parts, target)
                else:
                    attend(head, target)
        for index, head in enumerate(range(min(LEAD, stay), key_heads)):
            if OWN_WAVES[index] == wave:
                send_own(head)

    total = jnp.int32(0)
    for distance in range(chips):
        for way in (RIGHT, LEFT, FAR_RIGHT, FAR_LEFT):
            chip = place - distance if way in (RIGHT, FAR_RIGHT) else place + distance
            held = jnp.logical_and(chip >= 0, chip < chips)
            total = total + jnp.logical_and(held, sends(way, distance)).astype(jnp.int32)
    for count in range(1, n + 1):
        @pl.when(total == count)
        def _(count=count):
            pieces(key_heads, count, 0, recv_sem.at[0, 0]).wait_send()

    pieces(key_heads, chips, 1, sibling_recv.at[0]).wait_send()
    shipped = q_hbm.at[:, pl.ds(0, (key_heads - stay) * (head_width + 2 * HEAD_SIZE))]
    pltpu.make_async_remote_copy(
        src_ref=shipped, dst_ref=shipped, send_sem=ship_send, recv_sem=ship_recv.at[0],
        device_id=at_pipe(after), device_id_type=MESH,
    ).wait_send()
    done = pl.ds(0, stay * head_width)
    pltpu.make_async_remote_copy(
        src_ref=att.at[:, done], dst_ref=out_ref.at[:, done], send_sem=out_sem.at[0],
        recv_sem=out_sem.at[1], device_id=at_pipe(after), device_id_type=MESH,
    ).wait()


def write(parts, source, target, sem):
    share = source.shape[0] // parts
    copies = [
        pltpu.make_async_copy(
            source.at[pl.ds(i * share, share)], target.at[pl.ds(i * share, share)], sem.at[i]
        )
        for i in range(parts)
    ]
    for copy in copies:
        copy.start()
    for copy in copies:
        copy.wait()


def vmem_bytes(n, rows, width, kv_width):
    keys = n * rows
    gathered = 2 * keys * kv_width
    scores = 4 * rows * keys
    return gathered + 3 * 2 * rows * width + (5 * CHUNK + 2) * scores + 4 * 1024 * 1024


def on_device(queries, projected_key_value, layout):
    rows, width = queries.shape[2:]
    kv_width = projected_key_value.shape[3]
    key_heads = kv_width // (2 * HEAD_SIZE)
    per_kv = width // (key_heads * HEAD_SIZE)
    n = lax.axis_size("ctx")
    sections = lax.axis_size("pipe")
    arrived = pl.pallas_call(
        functools.partial(kernel, n, sections, key_heads, per_kv),
        out_shape=jax.ShapeDtypeStruct((rows, width), jnp.bfloat16),
        in_specs=[pl.BlockSpec(memory_space=pltpu.HBM)] * 3,
        out_specs=pl.BlockSpec(memory_space=pltpu.VMEM),
        scratch_shapes=[
            pltpu.VMEM((rows, width), jnp.bfloat16),
            pltpu.VMEM((key_heads, n, rows, 2 * HEAD_SIZE), jnp.bfloat16),
            pltpu.VMEM((rows, width), jnp.bfloat16),
            pltpu.VMEM((n, rows, rows), jnp.bfloat16),
            pltpu.VMEM((rows, rows), jnp.bfloat16),
            pltpu.SMEM(layout.shape, jnp.int32),
            pltpu.SemaphoreType.DMA,
            pltpu.SemaphoreType.DMA((2,)),
            pltpu.SemaphoreType.DMA((2,)),
            pltpu.SemaphoreType.DMA((key_heads, max(n // 2 - 1, 1))),
            pltpu.SemaphoreType.DMA((key_heads + len(SPLIT),)),
            pltpu.SemaphoreType.DMA((2,)),
            pltpu.SemaphoreType.DMA,
            pltpu.SemaphoreType.DMA((min(SHIP, key_heads - 1) + 1,)),
            pltpu.SemaphoreType.REGULAR,
        ],
        compiler_params=pltpu.CompilerParams(
            collective_id=0, has_side_effects=True, vmem_limit_bytes=vmem_bytes(n, rows, width, kv_width)
        ),
        name="gather_attend_relay",
    )(
        pltpu.with_memory_space_constraint(layout, pltpu.HBM),
        pltpu.with_memory_space_constraint(queries.reshape(rows, width), pltpu.HBM),
        pltpu.with_memory_space_constraint(
            projected_key_value.reshape(rows, kv_width), pltpu.HBM
        ),
    )
    parts = 1
    out = pl.pallas_call(
        functools.partial(write, parts),
        out_shape=jax.ShapeDtypeStruct((rows, width), jnp.bfloat16),
        in_specs=[pl.BlockSpec(memory_space=pltpu.VMEM)],
        out_specs=pl.BlockSpec(memory_space=pltpu.HBM),
        scratch_shapes=[pltpu.SemaphoreType.DMA((parts,))],
        compiler_params=pltpu.CompilerParams(vmem_limit_bytes=8 * 1024 * 1024),
        name="write_back",
    )(arrived)
    return out.reshape(queries.shape)


def solution(mesh):
    placed = (P("pipe", None, "ctx", None), P("pipe", None, "ctx", None), P())
    return jax.shard_map(
        on_device,
        mesh=mesh,
        in_specs=placed,
        out_specs=P("pipe", None, "ctx", None),
        check_vma=False,
    )
```
